256 devices in a mesh: tm: 64 (over y_hi, z, x), head: 4 (over y_lo, core).
Axes of the slice: x: 4, y: 4 (y_hi: 2, y_lo: 2; y = y_hi * 2 + y_lo), z: 8, core: 2. Of those that a mesh axis runs over, the one named last changes fastest.
Arguments:
- frames: bfloat16 [64, 512, 1152], P('tm', None, 'head'), may hold values from -6 to 6
- modulation: float32 [3, 1152], replicated, may hold values from -4 to 4
- w_qkv: bfloat16 [3, 1152, 1152], P(None, None, 'head'), may hold values from -1 to 1
- w_out: bfloat16 [1152, 1152], P('head'), may hold values from -0.375 to 0.375
- conv_taps: float32 [3, 1152], P(None, 'head'), may hold values from -3 to 3
- anchors: int32 [4], replicated, may hold values from 0 to 15
Outputs:
- block_out: bfloat16 [64, 512, 1152], P('tm', None, 'head')
The draws below stay inside these ranges and needn't reach their ends.
All inputs are finite; a program needn't handle non-finite values.
Results may differ from the reference program's by a relative error of at most 0.011.
Values may be sent and summed in bfloat16 or wider, within the bound.
A program may use at most 64 MiB of HBM per device.

```python
import jax
import jax.numpy as jnp
from jax import lax

D = 1152
HEADS = 16
HS = 72
P_SIZE = 512
SEG = 16
FRAMES = 64
SEGMENTS = 4


def draw_w_qkv(key, part):
    key_query, key_key, key_value = jax.random.split(key, 3)
    fan_scale = D ** (-0.5)
    w_query = jax.random.normal(key_query, (D, D), jnp.float32) * (1.5 * fan_scale)
    w_key = jax.random.normal(key_key, (D, D), jnp.float32) * (1.5 * fan_scale)
    w_value = jax.random.normal(key_value, (D, D), jnp.float32) * fan_scale
    stacked = jnp.stack([w_query, w_key, w_value])
    return jnp.clip(stacked, -1.0, 1.0).astype(jnp.bfloat16)


def plant(entries, stream_key, least, high):
    longest = entries.shape.index(max(entries.shape))
    spots = []
    for shift in (0, 1):
        where = [jax.random.randint(jax.random.fold_in(stream_key, axis), (), 0, length) for axis, length in enumerate(entries.shape)]
        where[longest] = (where[longest] + shift) % entries.shape[longest]
        spots.append(tuple(where))
    return entries.at[spots[0]].set(least).at[spots[1]].set(high)


def block_scale(own_key, extent, pieces, low, high):
    def one(position, parts):
        steps = jax.random.uniform(jax.random.fold_in(jax.random.fold_in(own_key, 6), position), (parts,), jnp.float32, low / len(pieces), high / len(pieces))
        return jnp.repeat(jnp.exp(steps), extent[position] // parts).reshape((-1,) + (1,) * (len(extent) - position - 1))

    loudness = one(*pieces[0])
    for cut in pieces[1:]:
        loudness = loudness * one(*cut)
    return loudness


def scatter_about(own_key, shape, deviation, bound, cuts=(), held_as=jnp.bfloat16):
    gain = block_scale(own_key, shape, cuts, -0.22, 0.18) if cuts else 1.0
    array = jax.random.normal(own_key, shape, jnp.float32) * deviation * gain
    return jnp.minimum(jnp.maximum(array, -bound), bound).astype(held_as)


def setup_inputs(seed: int = 0) -> dict:
    arg_keys = jax.random.split(jax.random.key(seed), 7)
    return {
        "frames": scatter_about(arg_keys[0], (FRAMES, P_SIZE, D), 1.0, 6.0, ((0, 64), (2, 4))),
        "modulation": scatter_about(arg_keys[1], (3, D), 0.8, 4.0, (), jnp.float32),
        "w_qkv": draw_w_qkv(jax.random.fold_in(arg_keys[6], 71), 0),
        "w_out": scatter_about(arg_keys[3], (D, D), (D // 4) ** -0.5, 0.375, ((0, 4),)),
        "conv_taps": scatter_about(arg_keys[4], (3, D), 0.5, 3.0, ((1, 4),), jnp.float32),
        "anchors": plant(jax.random.randint(arg_keys[5], (SEGMENTS,), 0, SEG), jax.random.fold_in(arg_keys[5], 1), 0, SEG - 1).astype(jnp.int32),
    }


EPSILON = 1e-06

def modulate(frame_rows, modulation):
    values = frame_rows.astype(jnp.float32)
    average = lax.optimization_barrier(jnp.mean(values, axis=-1, keepdims=True))
    centred = values - average
    variance = lax.optimization_barrier(jnp.mean(centred * centred, axis=-1, keepdims=True))
    normed = centred * lax.rsqrt(variance + EPSILON)
    return (normed * (1.0 + modulation[1]) + modulation[0]).astype(jnp.bfloat16)

def project_all(frame_rows, modulation, w_qkv):
    normed = modulate(frame_rows, modulation)
    return jnp.einsum('pd,cde->cpe', normed.astype(jnp.float32), w_qkv.astype(jnp.float32)).astype(jnp.bfloat16)

def attend(queries, key_rows, value_rows):
    scores = jnp.einsum('qhs,khs->hqk', queries.astype(jnp.float32), key_rows.astype(jnp.float32)) * HS ** (-0.5)
    row_max = lax.optimization_barrier(jnp.max(scores, axis=-1, keepdims=True))
    weights = jnp.exp(scores - row_max)
    weights = (weights / lax.optimization_barrier(jnp.sum(weights, axis=-1, keepdims=True))).astype(jnp.bfloat16)
    return jnp.einsum('hqk,khs->qhs', weights.astype(jnp.float32), value_rows.astype(jnp.float32)).astype(jnp.bfloat16)

def reference(frames, modulation, w_qkv, w_out, conv_taps, anchors):
    frame_count, tokens, width = frames.shape
    anchor_rows = (jnp.arange(SEGMENTS, dtype=jnp.int32) * SEG + anchors).astype(jnp.int32)

    def anchor_data(row):
        frame_rows = lax.dynamic_index_in_dim(frames, row, 0, keepdims=False)
        return project_all(frame_rows, modulation, w_qkv)[1:]
    anchor_pairs = lax.map(anchor_data, anchor_rows)

    def one_frame(frame_index):
        frame_rows = lax.dynamic_index_in_dim(frames, frame_index, 0, keepdims=False)
        triple = project_all(frame_rows, modulation, w_qkv)
        anchor_kv = lax.dynamic_index_in_dim(anchor_pairs, frame_index // SEG, 0, keepdims=False)
        key_rows = jnp.concatenate([triple[1], anchor_kv[0]], axis=0).reshape(2 * tokens, HEADS, HS)
        value_rows = jnp.concatenate([triple[2], anchor_kv[1]], axis=0).reshape(2 * tokens, HEADS, HS)
        attended = attend(triple[0].reshape(tokens, HEADS, HS), key_rows, value_rows).reshape(tokens, width)
        projected = jnp.dot(attended, w_out, preferred_element_type=jnp.float32)
        return (frame_rows.astype(jnp.float32) + modulation[2] * projected).astype(jnp.bfloat16)
    hidden = lax.map(one_frame, jnp.arange(frame_count, dtype=jnp.int32))
    padded = jnp.pad(hidden, ((1, 1), (0, 0), (0, 0))).astype(jnp.float32)
    block_out = padded[1:-1] + conv_taps[0] * padded[:-2] + conv_taps[1] * padded[1:-1] + conv_taps[2] * padded[2:]
    return block_out.astype(jnp.bfloat16)
```

```python
import jax
import jax.numpy as jnp
from jax import lax
from jax.experimental import pallas as pl
from jax.experimental.pallas import tpu as pltpu
from jax.sharding import PartitionSpec as P

HS = 72
SEG = 16
LINE = 4
EPSILON = 1e-06
PAD = 128
VROWS = 80
ROWS, COLS = 96, 128
LAG = 2
HALF = 256
MESH = pl.DeviceIdType.MESH
F32, BF16 = jnp.float32, jnp.bfloat16


def dot(a, b):
    return jnp.dot(a, b, preferred_element_type=F32)


def kernel(
    x_ref, mod_ref, wqkv_ref, wo_ref, taps_ref, anchors_ref, out_ref,
    xf, xa, zup, zdn, szup, szdn, base, xr, xl, sxr, sxl,
    modt, tapst, wot, qs, ks, vs, os_, ms, at,
    ps, pr, keep, ys, yr, hs, hl, hr,
    own_send, own_y, own_c, own_f,
    flow_send, up_recv, dn_recv, xr_recv, xl_recv,
    anc_send, anc_y, anc_c, anc_f,
    rs_send, rs_c, rs_y, halo_send, halo_l, halo_r,
):
    width, tokens = x_ref.shape
    heads = width // HS
    per_col = width // ROWS
    pieces = per_col * (tokens // COLS)
    halves = tokens // HALF
    d = xf.shape[0]
    tm, head = lax.axis_index("tm"), lax.axis_index("head")
    frames = lax.axis_size("tm")
    xpos = lax.rem(tm, LINE)
    zpos = lax.rem(tm // LINE, LINE)
    sib = head + 1 - 2 * lax.rem(head, 2)
    far = lax.rem(head + 2, 4)
    far_sib = lax.rem(sib + 2, 4)
    anchor = anchors_ref[tm // SEG]
    ax, az = lax.rem(anchor, LINE), anchor // LINE
    is_src = jnp.logical_and(ax == xpos, az == zpos)

    def remote(src, dst, send, recv, to_tm, to_head):
        return pltpu.make_async_remote_copy(
            src_ref=src, dst_ref=dst, send_sem=send, recv_sem=recv,
            device_id=(to_tm, to_head), device_id_type=MESH)

    barrier = pltpu.get_barrier_semaphore()

    def greet(to_tm, to_head):
        pl.semaphore_signal(barrier, inc=1, device_id=(to_tm, to_head), device_id_type=MESH)

    greet(tm, sib)
    greet(tm, far)
    links = ((tm > 0, tm - 1), (tm < frames - 1, tm + 1),
             (zpos > 0, tm - LINE), (zpos < LINE - 1, tm + LINE))
    count = jnp.int32(2)
    for there, who in links:
        @pl.when(there)
        def _(who=who):
            greet(who, head)
        count = count + there.astype(jnp.int32)
    pl.semaphore_wait(barrier, count)

    def rows_of(ref, j, cols):
        return ref.at[pl.ds(pl.multiple_of(j * width, 32), width), cols]

    def half(t):
        return pl.ds(t * HALF, HALF)

    def own_copy(t, to, send, recv):
        return remote(x_ref.at[:, half(t)], rows_of(xf, head, half(t)), send, recv, tm, to)

    def own_forward(t):
        return remote(rows_of(xf, far, half(t)), rows_of(xf, far, half(t)),
                      own_send.at[2, t], own_f.at[t], tm, sib)

    def own_start():
        for t in range(halves):
            own_copy(t, far, own_send.at[0, t], own_y.at[t]).start()
            own_copy(t, sib, own_send.at[1, t], own_c.at[t]).start()
        xf[pl.ds(pl.multiple_of(head * width, 32), width), :] = x_ref[...]

    def own_pass(t):
        own_copy(t, far, own_send.at[0, t], own_y.at[t]).wait_recv()
        own_forward(t).start()

    def piece(ref, p, off=0):
        f, c = lax.rem(p, per_col), p // per_col
        row = off + f * ROWS
        if not isinstance(row, int):
            row = pl.multiple_of(row, 32)
        col = c * COLS
        if not isinstance(col, int):
            col = pl.multiple_of(col, 128)
        return ref.at[pl.ds(row, ROWS), pl.ds(col, COLS)]

    def flow(s, place, stride, n, origin, src_here, got, sent, recv):
        p = s - LAG * place
        live = jnp.logical_and(p >= 0, p < pieces)
        nxt = tm + stride

        @pl.when(jnp.logical_and(live, place == 0))
        def _():
            remote(piece(origin, p), piece(got, p), flow_send.at[n], recv.at[p], nxt, head).start()

        @pl.when(jnp.logical_and(live, place > 0))
        def _():
            remote(piece(sent, p), piece(got, p), flow_send.at[n], recv.at[p], nxt, head).wait_recv()

            @pl.when(place < LINE - 1)
            def _():
                piece(sent, p)[...] = jnp.where(src_here, piece(origin, p)[...], piece(got, p)[...])
                remote(piece(sent, p), piece(got, p), flow_send.at[n], recv.at[p], nxt, head).start()

    def flow_end(place, stride, n, sent, recv):
        @pl.when(place < LINE - 1)
        def _():
            remote(sent, sent, flow_send.at[n], recv.at[0], tm + stride, head).wait_send()

    mine = head * width

    def anc_copy(p, to, send, recv):
        return remote(piece(xa, p, mine), piece(xa, p, mine), send, recv.at[p], tm, to)

    def anc_forward(p):
        return remote(piece(xa, p, far * width), piece(xa, p, far * width),
                      anc_send.at[2], anc_f.at[p], tm, sib)

    steps = pieces + 7 * LAG

    def step(s):
        flow(s, zpos, LINE, 0, x_ref, is_src, zup, szup, up_recv)
        flow(s, LINE - 1 - zpos, -LINE, 1, x_ref, is_src, zdn, szdn, dn_recv)
        p = s - 3 * LAG
        if 0 <= p < pieces:
            piece(base, p)[...] = jnp.where(
                is_src, piece(x_ref, p)[...],
                jnp.where(az < zpos, piece(zup, p)[...], piece(zdn, p)[...]))
        flow(p, xpos, 1, 2, base, ax == xpos, xr, sxr, xr_recv)
        flow(p, LINE - 1 - xpos, -1, 3, base, ax == xpos, xl, sxl, xl_recv)
        p = s - 6 * LAG
        if 0 <= p < pieces:
            piece(xa, p, mine)[...] = jnp.where(
                ax == xpos, piece(base, p)[...],
                jnp.where(ax < xpos, piece(xr, p)[...], piece(xl, p)[...]))
            anc_copy(p, far, anc_send.at[0], anc_y).start()
            anc_copy(p, sib, anc_send.at[1], anc_c).start()
        p = s - 7 * LAG
        if 0 <= p < pieces:
            anc_copy(p, far, anc_send.at[0], anc_y).wait_recv()
            anc_forward(p).start()

    def norm_project(src, t, first):
        v = src[:, half(t)].astype(F32)
        v = v - jnp.mean(v, axis=0, keepdims=True)
        r = lax.rsqrt(jnp.mean(v * v, axis=0, keepdims=True) + EPSILON)
        n = (v * r * (1.0 + modt[:, 1:2]) + modt[:, 0:1]).astype(BF16)
        return dot(wqkv_ref[first:, :], n)

    def put_kv(kv, t, offset):
        spot = pl.ds(offset + t * HALF, HALF)
        zeros = jnp.zeros((PAD - HS, HALF), F32)
        ones = jnp.where(lax.broadcasted_iota(jnp.int32, (VROWS - HS, HALF), 0) == 0, 1.0, 0.0)
        for h in range(heads):
            k = kv[h * HS:(h + 1) * HS]
            ks[h, spot, :] = jnp.concatenate([k, zeros], axis=0).T.astype(BF16)
            v = kv[width + h * HS:width + (h + 1) * HS]
            vs[h, :, spot] = jnp.concatenate([v, ones], axis=0).astype(BF16)

    def own_qkv(t):
        for wait in (own_copy(t, sib, own_send.at[1, t], own_c.at[t]), own_forward(t)):
            wait.wait_recv()
        qkv = norm_project(xf, t, 0)
        zeros = jnp.zeros((PAD - HS, HALF), F32)
        for h in range(heads):
            q = qkv[h * HS:(h + 1) * HS]
            qs[h, :, half(t)] = jnp.concatenate([q, zeros], axis=0).astype(BF16)
        put_kv(qkv[width:], t, 0)

    exponent = HS ** (-0.5) * 1.4426950408889634

    def attend_own(h, t):
        s = dot(ks[h, :tokens, :], qs[h, :, half(t)])
        m = jnp.max(s, axis=0, keepdims=True)
        p = jnp.exp2((s - m) * exponent).astype(BF16)
        os_[h, :, half(t)] = dot(vs[h, :, :tokens], p)
        ms[h, :, half(t)] = m

    def attend_anchor(h, t):
        s = dot(ks[h, tokens:, :], qs[h, :, half(t)])
        m0 = ms[h, :, half(t)]
        m = jnp.maximum(m0, jnp.max(s, axis=0, keepdims=True))
        p = jnp.exp2((s - m) * exponent).astype(BF16)
        o = os_[h, :, half(t)] * jnp.exp2((m0 - m) * exponent) + dot(vs[h, :, tokens:], p)
        at[h * HS:(h + 1) * HS, half(t)] = o[:HS] / o[HS:HS + 1]

    def rs_core(t, i):
        return remote(ps.at[i, :, half(t)], pr.at[i, :, half(t)],
                      rs_send.at[i, t], rs_c.at[i, t], tm, sib)

    def rs_far(t):
        return remote(ys.at[:, half(t)], yr.at[:, half(t)], rs_send.at[2, t], rs_y.at[t], tm, far)

    def project(t):
        a = at[:, half(t)].astype(BF16)

        def block(j):
            return dot(wot[pl.ds(pl.multiple_of(j * width, 32), width), :], a)

        for i, j in enumerate((far_sib, sib)):
            ps[1 - i, :, half(t)] = block(j).astype(BF16)
            rs_core(t, 1 - i).start()
        keep[1, :, half(t)] = block(far)
        keep[0, :, half(t)] = block(head)

    def sum_core(t):
        rs_core(t, 1).wait_recv()
        ys[:, half(t)] = (keep[1, :, half(t)] + pr[1, :, half(t)].astype(F32)).astype(BF16)
        rs_far(t).start()

    def halo_next(t):
        return remote(hs.at[:, half(t)], hl.at[:, half(t)], halo_send.at[0, t], halo_l.at[t], tm + 1, head)

    def halo_prev(t):
        return remote(hs.at[:, half(t)], hr.at[:, half(t)], halo_send.at[1, t], halo_r.at[t], tm - 1, head)

    has_next, has_prev = tm < frames - 1, tm > 0

    def sum_far(t):
        rs_core(t, 0).wait_recv()
        own = keep[0, :, half(t)] + pr[0, :, half(t)].astype(F32)
        rs_far(t).wait_recv()
        gate = modt[pl.ds(pl.multiple_of(head * width, 32), width), 2:3]
        total = own + yr[:, half(t)].astype(F32)
        hs[:, half(t)] = (x_ref[:, half(t)].astype(F32) + gate * total).astype(BF16)

        @pl.when(has_next)
        def _():
            halo_next(t).start()

        @pl.when(has_prev)
        def _():
            halo_prev(t).start()

    def finish(t):
        @pl.when(has_prev)
        def _():
            halo_next(t).wait_recv()

        @pl.when(has_next)
        def _():
            halo_prev(t).wait_recv()

        h = hs[:, half(t)].astype(F32)
        out_ref[:, half(t)] = (
            h + tapst[:, 0:1] * hl[:, half(t)].astype(F32)
            + tapst[:, 1:2] * h + tapst[:, 2:3] * hr[:, half(t)].astype(F32)
        ).astype(BF16)

    own_start()
    work = {}

    def after(s, fn, *args):
        work.setdefault(s, []).append((fn, args))

    def setup():
        modt[...] = mod_ref[...].T
        tapst[...] = taps_ref[...].T
        wot[...] = wo_ref[...].T

        @pl.when(jnp.logical_not(has_prev))
        def _():
            hl[...] = jnp.zeros_like(hl)

        @pl.when(jnp.logical_not(has_next))
        def _():
            hr[...] = jnp.zeros_like(hr)

    after(1, setup)
    after(6, own_pass, 0)
    after(9, own_qkv, 0)
    after(11, own_pass, 1)
    after(13, own_qkv, 1)
    units = [(h, t) for t in range(halves) for h in range(heads)]
    for i, (h, t) in enumerate(units):
        after(14 + i, attend_own, h, t)
    for s in range(steps):
        step(s)
        for fn, args in work.get(s, ()):
            fn(*args)

    def anchor_kv(t):
        for p in range(t * HALF // COLS * per_col, (t + 1) * HALF // COLS * per_col):
            anc_copy(p, sib, anc_send.at[1], anc_c).wait_recv()
            anc_forward(p).wait_recv()
        put_kv(norm_project(xa, t, width), t, tokens)

    for t in range(halves):
        anchor_kv(t)
    for h in range(heads):
        attend_anchor(h, 0)
    project(0)
    attend_anchor(0, 1)
    sum_core(0)
    for h in range(1, heads):
        attend_anchor(h, 1)
    project(1)
    sum_far(0)
    sum_core(1)
    finish(0)
    sum_far(1)
    finish(1)

    flow_end(zpos, LINE, 0, szup, up_recv)
    flow_end(LINE - 1 - zpos, -LINE, 1, szdn, dn_recv)
    flow_end(xpos, 1, 2, sxr, xr_recv)
    flow_end(LINE - 1 - xpos, -1, 3, sxl, xl_recv)
    shard = rows_of(xa, head, pl.ds(0, tokens))
    for n, to in ((0, far), (1, sib), (2, sib)):
        remote(shard, shard, anc_send.at[n], anc_y.at[0], tm, to).wait_send()
    for t in range(halves):
        own_copy(t, far, own_send.at[0, t], own_y.at[t]).wait_send()
        own_copy(t, sib, own_send.at[1, t], own_c.at[t]).wait_send()
        own_forward(t).wait_send()
        rs_core(t, 0).wait_send()
        rs_core(t, 1).wait_send()
        rs_far(t).wait_send()

        @pl.when(has_next)
        def _():
            halo_next(t).wait_send()

        @pl.when(has_prev)
        def _():
            halo_prev(t).wait_send()


def local(frames, modulation, w_qkv, w_out, conv_taps, anchors):
    _, tokens, width = frames.shape
    d = w_qkv.shape[1]
    heads = width // HS
    halves = tokens // HALF
    pieces = (width // ROWS) * (tokens // COLS)
    x_t = jnp.swapaxes(frames[0], 0, 1)
    w_t = jnp.swapaxes(w_qkv, 1, 2).reshape(3 * width, d)
    shard = pltpu.VMEM((width, tokens), BF16)
    dma = pltpu.SemaphoreType.DMA
    vmem = pl.BlockSpec(memory_space=pltpu.VMEM)
    out = pl.pallas_call(
        kernel,
        out_shape=jax.ShapeDtypeStruct((width, tokens), BF16),
        in_specs=[vmem] * 5 + [pl.BlockSpec(memory_space=pltpu.SMEM)],
        out_specs=vmem,
        scratch_shapes=[
            pltpu.VMEM((d, tokens), BF16), pltpu.VMEM((d, tokens), BF16),
            *[shard] * 9,
            pltpu.VMEM((d, 3), F32), pltpu.VMEM((width, 3), F32), pltpu.VMEM((d, width), BF16),
            pltpu.VMEM((heads, PAD, tokens), BF16),
            pltpu.VMEM((heads, 2 * tokens, PAD), BF16),
            pltpu.VMEM((heads, VROWS, 2 * tokens), BF16),
            pltpu.VMEM((heads, VROWS, tokens), F32),
            pltpu.VMEM((heads, 1, tokens), F32),
            pltpu.VMEM((width, tokens), F32),
            pltpu.VMEM((2, width, tokens), BF16), pltpu.VMEM((2, width, tokens), BF16),
            pltpu.VMEM((2, width, tokens), F32),
            *[shard] * 5,
            dma((3, halves)), dma((halves,)), dma((halves,)), dma((halves,)),
            dma((4,)), dma((pieces,)), dma((pieces,)), dma((pieces,)), dma((pieces,)),
            dma((3,)), dma((pieces,)), dma((pieces,)), dma((pieces,)),
            dma((3, halves)), dma((2, halves)), dma((halves,)),
            dma((2, halves)), dma((halves,)), dma((halves,)),
        ],
        compiler_params=pltpu.CompilerParams(
            collective_id=0, has_side_effects=True, vmem_limit_bytes=60 * 1024 * 1024),
        name="block",
    )(x_t, modulation, w_t, w_out, conv_taps, anchors)
    return jnp.swapaxes(out, 0, 1)[None]


def solution(mesh):
    in_specs = (
        P("tm", None, "head"),
        P(),
        P(None, None, "head"),
        P("head", None),
        P(None, "head"),
        P(),
    )
    out_specs = P("tm", None, "head")
    return jax.shard_map(local, mesh=mesh, in_specs=in_specs, out_specs=out_specs, check_vma=False)
```

```python
import jax
import jax.numpy as jnp
from jax import lax
from jax.experimental import pallas as pl
from jax.experimental.pallas import tpu as pltpu
from jax.sharding import PartitionSpec as P

HS = 72
SEG = 16
LINE = 4
EPSILON = 1e-06
PAD = 128
VROWS = 80
ROWS, COLS = 96, 256
LAG = 2
HALF = 256
MESH = pl.DeviceIdType.MESH
F32, BF16 = jnp.float32, jnp.bfloat16


def dot(a, b):
    return jnp.dot(a, b, preferred_element_type=F32)


def kernel(
    x_ref, mod_ref, wqkv_ref, wo_ref, taps_ref, anchors_ref, out_ref,
    xf, xa, zup, zdn, szup, szdn, base, xr, xl, sxr, sxl,
    modt, tapst, wot, qs, ks, vs, os_, ms, at,
    ps, pr, keep, ys, yr, hs, hl, hr,
    own_send, own_y, own_c, own_f,
    flow_send, up_recv, dn_recv, xr_recv, xl_recv,
    anc_send, anc_y, anc_c, anc_f,
    rs_send, rs_c, rs_y, halo_send, halo_l, halo_r,
):
    width, tokens = x_ref.shape
    heads = width // HS
    per_col = width // ROWS
    pieces = per_col * (tokens // COLS)
    halves = tokens // HALF
    d = xf.shape[0]
    tm, head = lax.axis_index("tm"), lax.axis_index("head")
    frames = lax.axis_size("tm")
    xpos = lax.rem(tm, LINE)
    zpos = lax.rem(tm // LINE, LINE)
    sib = head + 1 - 2 * lax.rem(head, 2)
    far = lax.rem(head + 2, 4)
    far_sib = lax.rem(sib + 2, 4)
    anchor = anchors_ref[tm // SEG]
    ax, az = lax.rem(anchor, LINE), anchor // LINE
    is_src = jnp.logical_and(ax == xpos, az == zpos)

    def remote(src, dst, send, recv, to_tm, to_head):
        return pltpu.make_async_remote_copy(
            src_ref=src, dst_ref=dst, send_sem=send, recv_sem=recv,
            device_id=(to_tm, to_head), device_id_type=MESH)

    barrier = pltpu.get_barrier_semaphore()

    def greet(to_tm, to_head):
        pl.semaphore_signal(barrier, inc=1, device_id=(to_tm, to_head), device_id_type=MESH)

    greet(tm, sib)
    greet(tm, far)
    links = ((tm > 0, tm - 1), (tm < frames - 1, tm + 1),
             (zpos > 0, tm - LINE), (zpos < LINE - 1, tm + LINE))
    count = jnp.int32(2)
    for there, who in links:
        @pl.when(there)
        def _(who=who):
            greet(who, head)
        count = count + there.astype(jnp.int32)
    pl.semaphore_wait(barrier, count)

    def rows_of(ref, j, cols):
        return ref.at[pl.ds(pl.multiple_of(j * width, 32), width), cols]

    def half(t):
        return pl.ds(t * HALF, HALF)

    def own_copy(t, to, send, recv):
        return remote(x_ref.at[:, half(t)], rows_of(xf, head, half(t)), send, recv, tm, to)

    def own_forward(t):
        return remote(rows_of(xf, far, half(t)), rows_of(xf, far, half(t)),
                      own_send.at[2, t], own_f.at[t], tm, sib)

    def own_start():
        for t in range(halves):
            own_copy(t, far, own_send.at[0, t], own_y.at[t]).start()
            own_copy(t, sib, own_send.at[1, t], own_c.at[t]).start()
        xf[pl.ds(pl.multiple_of(head * width, 32), width), :] = x_ref[...]

    def own_pass(t):
        own_copy(t, far, own_send.at[0, t], own_y.at[t]).wait_recv()
        own_forward(t).start()

    def piece(ref, p, off=0):
        f, c = lax.rem(p, per_col), p // per_col
        row = off + f * ROWS
        if not isinstance(row, int):
            row = pl.multiple_of(row, 32)
        col = c * COLS
        if not isinstance(col, int):
            col = pl.multiple_of(col, 128)
        return ref.at[pl.ds(row, ROWS), pl.ds(col, COLS)]

    def flow(s, place, stride, n, origin, src_here, got, sent, recv):
        p = s - LAG * place
        live = jnp.logical_and(p >= 0, p < pieces)
        nxt = tm + stride

        @pl.when(jnp.logical_and(live, place == 0))
        def _():
            remote(piece(origin, p), piece(got, p), flow_send.at[n], recv.at[p], nxt, head).start()

        @pl.when(jnp.logical_and(live, place > 0))
        def _():
            remote(piece(sent, p), piece(got, p), flow_send.at[n], recv.at[p], nxt, head).wait_recv()

            @pl.when(place < LINE - 1)
            def _():
                piece(sent, p)[...] = jnp.where(src_here, piece(origin, p)[...], piece(got, p)[...])
                remote(piece(sent, p), piece(got, p), flow_send.at[n], recv.at[p], nxt, head).start()

    def flow_end(place, stride, n, sent, recv):
        @pl.when(place < LINE - 1)
        def _():
            remote(sent, sent, flow_send.at[n], recv.at[0], tm + stride, head).wait_send()

    mine = head * width

    def anc_copy(p, to, send, recv):
        return remote(piece(xa, p, mine), piece(xa, p, mine), send, recv.at[p], tm, to)

    def anc_forward(p):
        return remote(piece(xa, p, far * width), piece(xa, p, far * width),
                      anc_send.at[2], anc_f.at[p], tm, sib)

    steps = pieces + 7 * LAG

    def step(s):
        flow(s, zpos, LINE, 0, x_ref, is_src, zup, szup, up_recv)
        flow(s, LINE - 1 - zpos, -LINE, 1, x_ref, is_src, zdn, szdn, dn_recv)
        p = s - 3 * LAG
        if 0 <= p < pieces:
            piece(base, p)[...] = jnp.where(
                is_src, piece(x_ref, p)[...],
                jnp.where(az < zpos, piece(zup, p)[...], piece(zdn, p)[...]))
        flow(p, xpos, 1, 2, base, ax == xpos, xr, sxr, xr_recv)
        flow(p, LINE - 1 - xpos, -1, 3, base, ax == xpos, xl, sxl, xl_recv)
        p = s - 6 * LAG
        if 0 <= p < pieces:
            piece(xa, p, mine)[...] = jnp.where(
                ax == xpos, piece(base, p)[...],
                jnp.where(ax < xpos, piece(xr, p)[...], piece(xl, p)[...]))
            anc_copy(p, far, anc_send.at[0], anc_y).start()
            anc_copy(p, sib, anc_send.at[1], anc_c).start()
        p = s - 7 * LAG
        if 0 <= p < pieces:
            anc_copy(p, far, anc_send.at[0], anc_y).wait_recv()
            anc_forward(p).start()

    def norm_project(src, t, first):
        v = src[:, half(t)].astype(F32)
        v = v - jnp.mean(v, axis=0, keepdims=True)
        r = lax.rsqrt(jnp.mean(v * v, axis=0, keepdims=True) + EPSILON)
        n = (v * r * (1.0 + modt[:, 1:2]) + modt[:, 0:1]).astype(BF16)
        return dot(wqkv_ref[first:, :], n)

    def put_kv(kv, t, offset):
        spot = pl.ds(offset + t * HALF, HALF)
        zeros = jnp.zeros((PAD - HS, HALF), F32)
        ones = jnp.where(lax.broadcasted_iota(jnp.int32, (VROWS - HS, HALF), 0) == 0, 1.0, 0.0)
        for h in range(heads):
            k = kv[h * HS:(h + 1) * HS]
            ks[h, spot, :] = jnp.concatenate([k, zeros], axis=0).T.astype(BF16)
            v = kv[width + h * HS:width + (h + 1) * HS]
            vs[h, :, spot] = jnp.concatenate([v, ones], axis=0).astype(BF16)

    def own_qkv(t):
        for wait in (own_copy(t, sib, own_send.at[1, t], own_c.at[t]), own_forward(t)):
            wait.wait_recv()
        qkv = norm_project(xf, t, 0)
        zeros = jnp.zeros((PAD - HS, HALF), F32)
        for h in range(heads):
            q = qkv[h * HS:(h + 1) * HS]
            qs[h, :, half(t)] = jnp.concatenate([q, zeros], axis=0).astype(BF16)
        put_kv(qkv[width:], t, 0)

    exponent = HS ** (-0.5) * 1.4426950408889634

    def attend(h, t, lo, size, first, last):
        keys = pl.ds(lo, size)
        s = dot(ks[h, keys, :], qs[h, :, half(t)])
        m = jnp.max(s, axis=0, keepdims=True)
        if not first:
            before = ms[h, :, half(t)]
            m = jnp.maximum(before, m)
        p = jnp.exp2((s - m) * exponent).astype(BF16)
        o = dot(vs[h, :, keys], p)
        if not first:
            o = os_[h, :, half(t)] * jnp.exp2((before - m) * exponent) + o
        if last:
            at[h * HS:(h + 1) * HS, half(t)] = o[:HS] / o[HS:HS + 1]
        else:
            os_[h, :, half(t)] = o
            ms[h, :, half(t)] = m

    def rs_core(t, i):
        return remote(ps.at[i, :, half(t)], pr.at[i, :, half(t)],
                      rs_send.at[i, t], rs_c.at[i, t], tm, sib)

    def rs_far(t):
        return remote(ys.at[:, half(t)], yr.at[:, half(t)], rs_send.at[2, t], rs_y.at[t], tm, far)

    def project(t):
        a = at[:, half(t)].astype(BF16)

        def block(j):
            return dot(wot[pl.ds(pl.multiple_of(j * width, 32), width), :], a)

        for i, j in enumerate((far_sib, sib)):
            ps[1 - i, :, half(t)] = block(j).astype(BF16)
            rs_core(t, 1 - i).start()
        keep[1, :, half(t)] = block(far)
        keep[0, :, half(t)] = block(head)

    def sum_core(t):
        rs_core(t, 1).wait_recv()
        ys[:, half(t)] = (keep[1, :, half(t)] + pr[1, :, half(t)].astype(F32)).astype(BF16)
        rs_far(t).start()

    def halo_next(t):
        return remote(hs.at[:, half(t)], hl.at[:, half(t)], halo_send.at[0, t], halo_l.at[t], tm + 1, head)

    def halo_prev(t):
        return remote(hs.at[:, half(t)], hr.at[:, half(t)], halo_send.at[1, t], halo_r.at[t], tm - 1, head)

    has_next, has_prev = tm < frames - 1, tm > 0

    def sum_far(t):
        rs_core(t, 0).wait_recv()
        own = keep[0, :, half(t)] + pr[0, :, half(t)].astype(F32)
        rs_far(t).wait_recv()
        gate = modt[pl.ds(pl.multiple_of(head * width, 32), width), 2:3]
        total = own + yr[:, half(t)].astype(F32)
        hs[:, half(t)] = (x_ref[:, half(t)].astype(F32) + gate * total).astype(BF16)

        @pl.when(has_next)
        def _():
            halo_next(t).start()

        @pl.when(has_prev)
        def _():
            halo_prev(t).start()

    def finish(t):
        @pl.when(has_prev)
        def _():
            halo_next(t).wait_recv()

        @pl.when(has_next)
        def _():
            halo_prev(t).wait_recv()

        h = hs[:, half(t)].astype(F32)
        out_ref[:, half(t)] = (
            h + tapst[:, 0:1] * hl[:, half(t)].astype(F32)
            + tapst[:, 1:2] * h + tapst[:, 2:3] * hr[:, half(t)].astype(F32)
        ).astype(BF16)

    own_start()
    work = {}

    def after(s, fn, *args):
        work.setdefault(s, []).append((fn, args))

    def setup():
        modt[...] = mod_ref[...].T
        tapst[...] = taps_ref[...].T
        wot[...] = wo_ref[...].T

        @pl.when(jnp.logical_not(has_prev))
        def _():
            hl[...] = jnp.zeros_like(hl)

        @pl.when(jnp.logical_not(has_next))
        def _():
            hr[...] = jnp.zeros_like(hr)

    def anchor_kv(t):
        for p in range(t * HALF // COLS * per_col, (t + 1) * HALF // COLS * per_col):
            anc_copy(p, sib, anc_send.at[1], anc_c).wait_recv()
            anc_forward(p).wait_recv()
        put_kv(norm_project(xa, t, width), t, tokens)

    units = [(h, t) for t in range(halves) for h in range(heads)]
    after(1, setup)
    after(3, own_pass, 0)
    after(5, own_pass, 1)
    after(5, own_qkv, 0)
    after(7, own_qkv, 1)
    for i, (h, t) in enumerate(units):
        after(8 + i, attend, h, t, 0, tokens, True, False)
    after(18, anchor_kv, 0)
    for i, (h, t) in enumerate(units):
        after(18 + i // 4, attend, h, t, tokens, HALF, False, False)
    for s in range(steps):
        step(s)
        for fn, args in work.get(s, ()):
            fn(*args)

    def last(h, t):
        attend(h, t, tokens + HALF, HALF, False, True)

    anchor_kv(1)
    for h in range(heads):
        last(h, 0)
    project(0)
    for h in range(heads - 1):
        last(h, 1)
    sum_core(0)
    last(heads - 1, 1)
    project(1)
    sum_core(1)
    for t in range(halves):
        sum_far(t)
    for t in range(halves):
        finish(t)

    flow_end(zpos, LINE, 0, szup, up_recv)
    flow_end(LINE - 1 - zpos, -LINE, 1, szdn, dn_recv)
    flow_end(xpos, 1, 2, sxr, xr_recv)
    flow_end(LINE - 1 - xpos, -1, 3, sxl, xl_recv)
    shard = rows_of(xa, head, pl.ds(0, tokens))
    for n, to in ((0, far), (1, sib), (2, sib)):
        remote(shard, shard, anc_send.at[n], anc_y.at[0], tm, to).wait_send()
    for t in range(halves):
        own_copy(t, far, own_send.at[0, t], own_y.at[t]).wait_send()
        own_copy(t, sib, own_send.at[1, t], own_c.at[t]).wait_send()
        own_forward(t).wait_send()
        rs_core(t, 0).wait_send()
        rs_core(t, 1).wait_send()
        rs_far(t).wait_send()

        @pl.when(has_next)
        def _():
            halo_next(t).wait_send()

        @pl.when(has_prev)
        def _():
            halo_prev(t).wait_send()


def local(frames, modulation, w_qkv, w_out, conv_taps, anchors):
    _, tokens, width = frames.shape
    d = w_qkv.shape[1]
    heads = width // HS
    halves = tokens // HALF
    pieces = (width // ROWS) * (tokens // COLS)
    x_t = jnp.swapaxes(frames[0], 0, 1)
    w_t = jnp.swapaxes(w_qkv, 1, 2).reshape(3 * width, d)
    shard = pltpu.VMEM((width, tokens), BF16)
    dma = pltpu.SemaphoreType.DMA
    vmem = pl.BlockSpec(memory_space=pltpu.VMEM)
    out = pl.pallas_call(
        kernel,
        out_shape=jax.ShapeDtypeStruct((width, tokens), BF16),
        in_specs=[vmem] * 5 + [pl.BlockSpec(memory_space=pltpu.SMEM)],
        out_specs=vmem,
        scratch_shapes=[
            pltpu.VMEM((d, tokens), BF16), pltpu.VMEM((d, tokens), BF16),
            *[shard] * 9,
            pltpu.VMEM((d, 3), F32), pltpu.VMEM((width, 3), F32), pltpu.VMEM((d, width), BF16),
            pltpu.VMEM((heads, PAD, tokens), BF16),
            pltpu.VMEM((heads, 2 * tokens, PAD), BF16),
            pltpu.VMEM((heads, VROWS, 2 * tokens), BF16),
            pltpu.VMEM((heads, VROWS, tokens), F32),
            pltpu.VMEM((heads, 1, tokens), F32),
            pltpu.VMEM((width, tokens), F32),
            pltpu.VMEM((2, width, tokens), BF16), pltpu.VMEM((2, width, tokens), BF16),
            pltpu.VMEM((2, width, tokens), F32),
            *[shard] * 5,
            dma((3, halves)), dma((halves,)), dma((halves,)), dma((halves,)),
            dma((4,)), dma((pieces,)), dma((pieces,)), dma((pieces,)), dma((pieces,)),
            dma((3,)), dma((pieces,)), dma((pieces,)), dma((pieces,)),
            dma((3, halves)), dma((2, halves)), dma((halves,)),
            dma((2, halves)), dma((halves,)), dma((halves,)),
        ],
        compiler_params=pltpu.CompilerParams(
            collective_id=0, has_side_effects=True, vmem_limit_bytes=60 * 1024 * 1024),
        name="block",
    )(x_t, modulation, w_t, w_out, conv_taps, anchors)
    return jnp.swapaxes(out, 0, 1)[None]


def solution(mesh):
    in_specs = (
        P("tm", None, "head"),
        P(),
        P(None, None, "head"),
        P("head", None),
        P(None, "head"),
        P(),
    )
    out_specs = P("tm", None, "head")
    return jax.shard_map(local, mesh=mesh, in_specs=in_specs, out_specs=out_specs, check_vma=False)
```

```python
import jax
import jax.numpy as jnp
from jax import lax
from jax.experimental import pallas as pl
from jax.experimental.pallas import tpu as pltpu
from jax.sharding import PartitionSpec as P

HS = 72
SEG = 16
LINE = 4
EPSILON = 1e-06
PAD = 128
VROWS = 80
COLS = 128
PARTS = 2
HALF = 256
MESH = pl.DeviceIdType.MESH
F32, BF16 = jnp.float32, jnp.bfloat16


def dot(a, b):
    return jnp.dot(a, b, preferred_element_type=F32)


def kernel(
    x_ref, mod_ref, wqkv_ref, wo_ref, taps_ref, anchors_ref, out_ref,
    xf, xa, got_x, here_x, got_z,
    modt, tapst, wot, qs, ks, vs, os_, ms, at,
    ps, pr, keep, ys, yr, hs, hl, hr,
    own_send, own_y, own_c, own_f,
    row_send, row_recv, col_send, col_recv, all_send, all_recv,
    anc_send, anc_y, anc_c, anc_f,
    rs_send, rs_c, rs_y, halo_send, halo_l, halo_r,
):
    width, tokens = x_ref.shape
    heads = width // HS
    rows = width // PARTS
    halves = tokens // HALF
    d = xf.shape[0]
    tm, head = lax.axis_index("tm"), lax.axis_index("head")
    frames = lax.axis_size("tm")
    xpos = lax.rem(tm, LINE)
    zpos = lax.rem(tm // LINE, LINE)
    sib = head + 1 - 2 * lax.rem(head, 2)
    far = lax.rem(head + 2, 4)
    far_sib = lax.rem(sib + 2, 4)
    anchor = anchors_ref[tm // SEG]
    ax, az = lax.rem(anchor, LINE), anchor // LINE
    from_x, from_z = lax.rem(xpos - ax + LINE, LINE), lax.rem(zpos - az + LINE, LINE)

    def remote(src, dst, send, recv, to_tm, to_head):
        return pltpu.make_async_remote_copy(
            src_ref=src, dst_ref=dst, send_sem=send, recv_sem=recv,
            device_id=(to_tm, to_head), device_id_type=MESH)

    barrier = pltpu.get_barrier_semaphore()

    def greet(to_tm, to_head):
        pl.semaphore_signal(barrier, inc=1, device_id=(to_tm, to_head), device_id_type=MESH)

    greet(tm, sib)
    greet(tm, far)
    def in_row(k):
        return tm - xpos + lax.rem(xpos + k, LINE)

    def in_column(k):
        return tm + LINE * (lax.rem(zpos + k, LINE) - zpos)

    for k in range(1, LINE):
        greet(in_row(k), head)
        greet(in_column(k), head)
    count = jnp.int32(2 * LINE)
    for there, who in ((tm > 0, tm - 1), (tm < frames - 1, tm + 1)):
        @pl.when(there)
        def _(who=who):
            greet(who, head)
        count = count + there.astype(jnp.int32)
    pl.semaphore_wait(barrier, count)

    def rows_of(ref, j, cols):
        return ref.at[pl.ds(pl.multiple_of(j * width, 32), width), cols]

    def half(t):
        return pl.ds(t * HALF, HALF)

    def own_copy(t, to, send, recv):
        return remote(x_ref.at[:, half(t)], rows_of(xf, head, half(t)), send, recv, tm, to)

    def own_forward(t):
        return remote(rows_of(xf, far, half(t)), rows_of(xf, far, half(t)),
                      own_send.at[2, t], own_f.at[t], tm, sib)

    def own_start():
        for t in range(halves):
            own_copy(t, far, own_send.at[0, t], own_y.at[t]).start()
            own_copy(t, sib, own_send.at[1, t], own_c.at[t]).start()
        xf[pl.ds(pl.multiple_of(head * width, 32), width), :] = x_ref[...]

    def own_pass(t):
        own_copy(t, far, own_send.at[0, t], own_y.at[t]).wait_recv()
        own_forward(t).start()

    def part(u):
        return pl.ds(u * rows, rows)

    def quarter(j):
        return pl.ds(pl.multiple_of(j * COLS, COLS), COLS)

    def row_copy(u, k):
        return remote(x_ref.at[part(u), quarter(lax.rem(xpos + k, LINE))], got_x.at[k - 1, part(u), :],
                      row_send.at[u, k - 1], row_recv.at[u, k - 1], in_row(k), head)

    def column_copy(u, k):
        return remote(here_x.at[part(u), :], got_z.at[k - 1, part(u), :],
                      col_send.at[u, k - 1], col_recv.at[u, k - 1], in_column(k), head)

    def block(k, u, j):
        return xa.at[k, pl.ds(pl.multiple_of(j * width + u * rows, 16), rows), :]

    def all_copy(u, k):
        return remote(block(0, u, head), block(k, u, head),
                      all_send.at[u, k - 1], all_recv.at[u, k - 1], in_row(k), head)

    def anc_copy(u, k, to, n, recv):
        return remote(block(k, u, head), block(k, u, head), anc_send.at[n, u, k], recv.at[u, k], tm, to)

    def anc_forward(u, k):
        return remote(block(k, u, far), block(k, u, far), anc_send.at[2, u, k], anc_f.at[u, k], tm, sib)

    others = (2, 1, 3)

    def row_start():
        for u in range(PARTS):
            for k in others:
                row_copy(u, k).start()

    def pick(which, own, got, u):
        for k in range(1, LINE):
            own = jnp.where(which == k, got[k - 1, part(u), :], own)
        return own

    def row_pick(u):
        for k in others:
            row_copy(u, k).wait_recv()
        here_x[part(u), :] = pick(from_x, x_ref[part(u), quarter(xpos)], got_x, u)
        for k in others:
            column_copy(u, k).start()

    def share(u, k):
        anc_copy(u, k, far, 0, anc_y).start()
        anc_copy(u, k, sib, 1, anc_c).start()

    def column_pick(u):
        for k in others:
            column_copy(u, k).wait_recv()
        block(0, u, head)[...] = pick(from_z, here_x[part(u), :], got_z, u)
        for k in others:
            all_copy(u, k).start()
        share(u, 0)

    def all_pass(u, k):
        all_copy(u, k).wait_recv()
        share(u, k)

    def anc_pass(u, k):
        anc_copy(u, k, far, 0, anc_y).wait_recv()
        anc_forward(u, k).start()

    def norm_project(v, first):
        v = v.astype(F32)
        v = v - jnp.mean(v, axis=0, keepdims=True)
        r = lax.rsqrt(jnp.mean(v * v, axis=0, keepdims=True) + EPSILON)
        n = (v * r * (1.0 + modt[:, 1:2]) + modt[:, 0:1]).astype(BF16)
        return dot(wqkv_ref[first:, :], n)

    def put_kv(kv, t, offset):
        spot = pl.ds(offset + t * HALF, HALF)
        zeros = jnp.zeros((PAD - HS, HALF), F32)
        ones = jnp.where(lax.broadcasted_iota(jnp.int32, (VROWS - HS, HALF), 0) == 0, 1.0, 0.0)
        for h in range(heads):
            k = kv[h * HS:(h + 1) * HS]
            ks[h, spot, :] = jnp.concatenate([k, zeros], axis=0).T.astype(BF16)
            v = kv[width + h * HS:width + (h + 1) * HS]
            vs[h, :, spot] = jnp.concatenate([v, ones], axis=0).astype(BF16)

    def own_qkv(t):
        for wait in (own_copy(t, sib, own_send.at[1, t], own_c.at[t]), own_forward(t)):
            wait.wait_recv()
        qkv = norm_project(xf[:, half(t)], 0)
        zeros = jnp.zeros((PAD - HS, HALF), F32)
        for h in range(heads):
            q = qkv[h * HS:(h + 1) * HS]
            qs[h, :, half(t)] = jnp.concatenate([q, zeros], axis=0).astype(BF16)
        put_kv(qkv[width:], t, 0)

    exponent = HS ** (-0.5) * 1.4426950408889634

    def attend(h, t, lo, size, first, last):
        keys = pl.ds(lo, size)
        s = dot(ks[h, keys, :], qs[h, :, half(t)])
        m = jnp.max(s, axis=0, keepdims=True)
        if not first:
            before = ms[h, :, half(t)]
            m = jnp.maximum(before, m)
        p = jnp.exp2((s - m) * exponent).astype(BF16)
        o = dot(vs[h, :, keys], p)
        if not first:
            o = os_[h, :, half(t)] * jnp.exp2((before - m) * exponent) + o
        if last:
            at[h * HS:(h + 1) * HS, half(t)] = o[:HS] / o[HS:HS + 1]
        else:
            os_[h, :, half(t)] = o
            ms[h, :, half(t)] = m

    def rs_core(t, i):
        return remote(ps.at[i, :, half(t)], pr.at[i, :, half(t)],
                      rs_send.at[i, t], rs_c.at[i, t], tm, sib)

    def rs_far(t):
        return remote(ys.at[:, half(t)], yr.at[:, half(t)], rs_send.at[2, t], rs_y.at[t], tm, far)

    def project(t):
        a = at[:, half(t)].astype(BF16)

        def block(j):
            return dot(wot[pl.ds(pl.multiple_of(j * width, 32), width), :], a)

        for i, j in enumerate((far_sib, sib)):
            ps[1 - i, :, half(t)] = block(j).astype(BF16)
            rs_core(t, 1 - i).start()
        keep[1, :, half(t)] = block(far)
        keep[0, :, half(t)] = block(head)

    def sum_core(t):
        rs_core(t, 1).wait_recv()
        ys[:, half(t)] = (keep[1, :, half(t)] + pr[1, :, half(t)].astype(F32)).astype(BF16)
        rs_far(t).start()

    def halo_next(t):
        return remote(hs.at[:, half(t)], hl.at[:, half(t)], halo_send.at[0, t], halo_l.at[t], tm + 1, head)

    def halo_prev(t):
        return remote(hs.at[:, half(t)], hr.at[:, half(t)], halo_send.at[1, t], halo_r.at[t], tm - 1, head)

    has_next, has_prev = tm < frames - 1, tm > 0

    def sum_far(t):
        rs_core(t, 0).wait_recv()
        own = keep[0, :, half(t)] + pr[0, :, half(t)].astype(F32)
        rs_far(t).wait_recv()
        gate = modt[pl.ds(pl.multiple_of(head * width, 32), width), 2:3]
        total = own + yr[:, half(t)].astype(F32)
        hs[:, half(t)] = (x_ref[:, half(t)].astype(F32) + gate * total).astype(BF16)

        @pl.when(has_next)
        def _():
            halo_next(t).start()

        @pl.when(has_prev)
        def _():
            halo_prev(t).start()

    def finish(t):
        @pl.when(has_prev)
        def _():
            halo_next(t).wait_recv()

        @pl.when(has_next)
        def _():
            halo_prev(t).wait_recv()

        h = hs[:, half(t)].astype(F32)
        out_ref[:, half(t)] = (
            h + tapst[:, 0:1] * hl[:, half(t)].astype(F32)
            + tapst[:, 1:2] * h + tapst[:, 2:3] * hr[:, half(t)].astype(F32)
        ).astype(BF16)

    own_start()
    row_start()
    def setup():
        modt[...] = mod_ref[...].T
        tapst[...] = taps_ref[...].T
        wot[...] = wo_ref[...].T

        @pl.when(jnp.logical_not(has_prev))
        def _():
            hl[...] = jnp.zeros_like(hl)

        @pl.when(jnp.logical_not(has_next))
        def _():
            hr[...] = jnp.zeros_like(hr)

    order = (0, 1, 3, 2)
    per_half = HALF // COLS

    def anchor_kv(t):
        ks_of = order[t * per_half:(t + 1) * per_half]
        for k in ks_of:
            for u in range(PARTS):
                anc_copy(u, k, sib, 1, anc_c).wait_recv()
                anc_forward(u, k).wait_recv()
        v = jnp.concatenate([xa[k] for k in ks_of], axis=1)
        put_kv(norm_project(v, width), t, tokens)

    units = [(h, t) for t in range(halves) for h in range(heads)]

    def own_units(lo, hi):
        for h, t in units[lo:hi]:
            attend(h, t, 0, tokens, True, False)

    setup()
    row_pick(0)
    own_pass(0)
    row_pick(1)
    own_qkv(0)
    own_pass(1)
    own_qkv(1)
    own_units(0, 4)
    column_pick(0)
    own_units(4, 8)
    column_pick(1)
    anc_pass(0, 0)
    for k in order[1:]:
        all_pass(0, k)
    anc_pass(1, 0)
    all_pass(1, 1)
    anc_pass(0, 1)
    all_pass(1, 3)
    anc_pass(0, 3)
    all_pass(1, 2)
    anc_pass(0, 2)
    anc_pass(1, 1)
    anc_pass(1, 3)
    anc_pass(1, 2)
    anchor_kv(0)
    for h, t in units:
        attend(h, t, tokens, HALF, False, False)

    def last(h, t):
        attend(h, t, tokens + HALF, HALF, False, True)

    anchor_kv(1)
    for h in range(heads):
        last(h, 0)
    project(0)
    for h in range(heads - 1):
        last(h, 1)
    sum_core(0)
    last(heads - 1, 1)
    project(1)
    sum_core(1)
    for t in range(halves):
        sum_far(t)
    for t in range(halves):
        finish(t)

    for u in range(PARTS):
        for k in others:
            row_copy(u, k).wait_send()
            column_copy(u, k).wait_send()
            all_copy(u, k).wait_send()
        for k in range(LINE):
            anc_copy(u, k, far, 0, anc_y).wait_send()
            anc_copy(u, k, sib, 1, anc_c).wait_send()
            anc_forward(u, k).wait_send()
    for t in range(halves):
        own_copy(t, far, own_send.at[0, t], own_y.at[t]).wait_send()
        own_copy(t, sib, own_send.at[1, t], own_c.at[t]).wait_send()
        own_forward(t).wait_send()
        rs_core(t, 0).wait_send()
        rs_core(t, 1).wait_send()
        rs_far(t).wait_send()

        @pl.when(has_next)
        def _():
            halo_next(t).wait_send()

        @pl.when(has_prev)
        def _():
            halo_prev(t).wait_send()


def local(frames, modulation, w_qkv, w_out, conv_taps, anchors):
    _, tokens, width = frames.shape
    d = w_qkv.shape[1]
    heads = width // HS
    halves = tokens // HALF
    x_t = jnp.swapaxes(frames[0], 0, 1)
    w_t = jnp.swapaxes(w_qkv, 1, 2).reshape(3 * width, d)
    shard = pltpu.VMEM((width, tokens), BF16)
    dma = pltpu.SemaphoreType.DMA
    vmem = pl.BlockSpec(memory_space=pltpu.VMEM)
    out = pl.pallas_call(
        kernel,
        out_shape=jax.ShapeDtypeStruct((width, tokens), BF16),
        in_specs=[vmem] * 5 + [pl.BlockSpec(memory_space=pltpu.SMEM)],
        out_specs=vmem,
        scratch_shapes=[
            pltpu.VMEM((d, tokens), BF16), pltpu.VMEM((LINE, d, COLS), BF16),
            pltpu.VMEM((LINE - 1, width, COLS), BF16), pltpu.VMEM((width, COLS), BF16),
            pltpu.VMEM((LINE - 1, width, COLS), BF16),
            pltpu.VMEM((d, 3), F32), pltpu.VMEM((width, 3), F32), pltpu.VMEM((d, width), BF16),
            pltpu.VMEM((heads, PAD, tokens), BF16),
            pltpu.VMEM((heads, 2 * tokens, PAD), BF16),
            pltpu.VMEM((heads, VROWS, 2 * tokens), BF16),
            pltpu.VMEM((heads, VROWS, tokens), F32),
            pltpu.VMEM((heads, 1, tokens), F32),
            pltpu.VMEM((width, tokens), F32),
            pltpu.VMEM((2, width, tokens), BF16), pltpu.VMEM((2, width, tokens), BF16),
            pltpu.VMEM((2, width, tokens), F32),
            *[shard] * 5,
            dma((3, halves)), dma((halves,)), dma((halves,)), dma((halves,)),
            *[dma((PARTS, LINE - 1))] * 6,
            dma((3, PARTS, LINE)), *[dma((PARTS, LINE))] * 3,
            dma((3, halves)), dma((2, halves)), dma((halves,)),
            dma((2, halves)), dma((halves,)), dma((halves,)),
        ],
        compiler_params=pltpu.CompilerParams(
            collective_id=0, has_side_effects=True, vmem_limit_bytes=60 * 1024 * 1024),
        name="block",
    )(x_t, modulation, w_t, w_out, conv_taps, anchors)
    return jnp.swapaxes(out, 0, 1)[None]


def solution(mesh):
    in_specs = (
        P("tm", None, "head"),
        P(),
        P(None, None, "head"),
        P("head", None),
        P(None, "head"),
        P(),
    )
    out_specs = P("tm", None, "head")
    return jax.shard_map(local, mesh=mesh, in_specs=in_specs, out_specs=out_specs, check_vma=False)
```
